32 devices in a mesh: groups: 2 (over x), view: 16 (over z, y, core).
Axes of the slice: x: 2, y: 2, z: 4, core: 2. Of those that a mesh axis runs over, the one named last changes fastest.
Arguments:
- ref_features: bfloat16 [256, 32, 384], P(('groups', 'view')), parts along dimension 0, may hold values from -6 to 6
- source_tiles: bfloat16 [1024, 2, 32, 384], P(('groups', 'view')), parts along dimension 0, may hold values from -6 to 6
- pair_lists: int32 [32, 4, 4], P(('groups', 'view')), parts along dimension 0, may hold values from -1 to 511, as said below
- view_counts: int32 [32], P(('groups', 'view')), parts along dimension 0, may hold values from 3 to 4, as said below
- disparities: int32 [16, 4], P('groups'), parts along dimension 0, may hold values from -48 to 48
- conv_first: bfloat16 [3, 3, 8, 3, 32], replicated, may hold values from -0.21875 to 0.21875
- bias_first: float32 [8], replicated, may hold values from -3 to 3
- conv_second: bfloat16 [16, 3, 3, 3, 8], replicated, may hold values from -0.4375 to 0.4375
- bias_second: float32 [16], replicated, may hold values from -3 to 3
Outputs:
- cost_features: float32 [8, 64, 16, 192], P('groups', 'view'), parts along dimension 0
The draws below stay inside these ranges and needn't reach their ends.
There are 2 independent parts, one for each index of `groups`. The reference program is written for one: setup_inputs(seed, part) draws one part's arguments, and reference() takes and returns one part's arrays. A program takes and returns all parts, laid end to end along the dimension named above; an argument that names none is the same for every part. Nothing has to cross between parts.
Inputs may be any that keep to these rules, and one draw needn't show every extreme that they name: pair_lists[v, s, b] is the tile holding rows 2b and 2b + 1 of source s of strip v; it is -1 exactly when s >= view_counts[v]; tile t lies on device t // 32 of the view axis; no strip takes more than 2 tiles from one device, and some strip takes exactly 2 from some device. `view_counts`: some strip uses 3 sources and some uses 4.
All inputs are finite; a program needn't handle non-finite values.
Results may differ from the reference program's by a relative error of at most 0.0028.
Values may be sent and summed in bfloat16 or wider, within the bound.
A program may use at most 128 MiB of HBM per device.

```python
import jax
import jax.numpy as jnp
from jax import lax

C = 32
C1 = 8
C2 = 16
COLS = 384
ROWS = 8
PLANES = 8
SOURCES = 4
SHIFT = 48
TILES_DEV = 32
STRIPS = 16
TILES = 512
HEIGHT = 128
BLOCKS = 4
CAP = 2


def survey_pairs(key):
    base_key = jax.random.fold_in(key, 7331)
    key_count, key_pick, key_pop, key_rows = jax.random.split(base_key, 4)
    view_counts = jax.random.randint(key_count, (STRIPS,), 3, 5)
    full_strip = jax.random.randint(key_pick, (), 0, STRIPS)
    strip_ids = jnp.arange(STRIPS)
    view_counts = jnp.where(strip_ids == full_strip, 4, view_counts)
    view_counts = jnp.where(strip_ids == (full_strip + 1) % STRIPS, 3, view_counts)
    popular = jax.random.randint(key_pop, (STRIPS,), 0, 4) * (STRIPS // 2 + 1)
    requests = SOURCES * BLOCKS
    least_full = max(-((STRIPS - requests) // (CAP - 1)), 1)
    most_full = requests // CAP

    def one_strip(strip_key):
        key_jitter, key_shuffle, key_tile, key_twins = jax.random.split(strip_key, 4)
        jitter = jax.random.randint(key_jitter, (STRIPS,), 0, 2 * STRIPS)
        ranking = popular + jitter
        ranked = jnp.argsort(-ranking, stable=True)
        full_count = jax.random.randint(key_twins, (), least_full, most_full + 1)
        shuffled = jax.random.permutation(key_shuffle, requests)
        owner_slot = jnp.where(shuffled < CAP * full_count, shuffled // CAP, shuffled - CAP * full_count + full_count)
        owners = ranked[owner_slot]
        local_ids = jax.random.randint(key_tile, (requests,), 0, TILES_DEV)
        return owners * TILES_DEV + local_ids
    tile_ids = jax.vmap(one_strip)(jax.random.split(key_rows, STRIPS)).reshape(STRIPS, SOURCES, BLOCKS)
    source_ids = jnp.arange(SOURCES)
    in_use = source_ids[None, :, None] < view_counts[:, None, None]
    pair_ids = jnp.where(in_use, tile_ids, -1)
    return (pair_ids.astype(jnp.int32), view_counts.astype(jnp.int32))


def draw_pair_lists(key, part):
    return survey_pairs(key)[0]


def draw_view_counts(key, part):
    return survey_pairs(key)[1]


def touch_ends(result, own_key, low, top_value):
    extent = result.shape
    spot = [jax.random.randint(jax.random.fold_in(own_key, axis), (), 0, extent[axis]) for axis in range(len(extent))]
    result = result.at[tuple(spot)].set(low)
    longest = extent.index(max(extent))
    spot[longest] = (spot[longest] + 1) % extent[longest]
    return result.at[tuple(spot)].set(top_value)


def block_scale(own_key, extent, cuts, low, largest):
    loudness, own = 1.0, jax.random.fold_in(own_key, 6)
    for axis_at, blocks in cuts:
        draws = jnp.exp(jax.random.uniform(jax.random.fold_in(own, axis_at), (blocks,), jnp.float32, low / len(cuts), largest / len(cuts)))
        loudness = loudness * jnp.repeat(draws, extent[axis_at] // blocks).reshape([-1 if axis == axis_at else 1 for axis in range(len(extent))])
    return loudness


def bell_draw(stream_key, shape, width, bound, pieces=(), held_as=jnp.bfloat16):
    values = width * jax.random.normal(stream_key, shape, jnp.float32)
    if pieces:
        values = values * block_scale(stream_key, shape, pieces, -0.22, 0.18)
    return jnp.clip(values, -bound, bound).astype(held_as)


def setup_inputs(seed: int = 0, part: int = 0) -> dict:
    splits = jax.random.split(jax.random.key(seed), 10)
    part_splits = jax.random.split(jax.random.fold_in(splits[9], part), 10)
    return {
        "ref_features": bell_draw(part_splits[0], (HEIGHT, C, COLS), 1.0, 6.0, ((0, 16),)),
        "source_tiles": bell_draw(part_splits[1], (TILES, 2, C, COLS), 1.0, 6.0, ((0, 16),)),
        "pair_lists": draw_pair_lists(jax.random.fold_in(jax.random.fold_in(splits[9], part), 71), part),
        "view_counts": draw_view_counts(jax.random.fold_in(jax.random.fold_in(splits[9], part), 71), part),
        "disparities": touch_ends(jax.random.randint(part_splits[4], (PLANES, SOURCES), 0 - SHIFT, SHIFT + 1), jax.random.fold_in(part_splits[4], 1), 0 - SHIFT, SHIFT).astype(jnp.int32),
        "conv_first": bell_draw(splits[5], (3, 3, C1, 3, C), (27 * C) ** -0.5, 0.21875),
        "bias_first": bell_draw(splits[6], (C1,), 0.5, 3.0, (), jnp.float32),
        "conv_second": bell_draw(splits[7], (C2, 3, 3, 3, C1), (27 * C1) ** -0.5, 0.4375),
        "bias_second": bell_draw(splits[8], (C2,), 0.5, 3.0, (), jnp.float32),
    }


def shifted(rows, offset):
    padded = jnp.pad(rows, ((0, 0), (0, 0), (SHIFT, SHIFT)))
    return lax.dynamic_slice_in_dim(padded, (SHIFT - offset).astype(jnp.int32), COLS, 2)


def strip_variance(ref_rows, pair_row, live_count, source_tiles, disparities):
    ref_wide = ref_rows.astype(jnp.float32)
    summed = jnp.broadcast_to(ref_wide, (PLANES,) + ref_wide.shape)
    squares = summed * summed
    for source in range(SOURCES):
        picked = source_tiles[jnp.maximum(pair_row[source], 0)].reshape(ROWS, C, COLS)
        warped = jax.vmap(lambda offset: shifted(picked, offset))(disparities[:, source]).astype(jnp.float32)
        weight = (source < live_count).astype(jnp.float32)
        summed = summed + weight * warped
        squares = squares + weight * warped * warped
    view_total = live_count.astype(jnp.float32) + 1.0
    view_mean = summed / view_total
    return (squares / view_total - view_mean * view_mean).astype(jnp.bfloat16)


def reference(ref_features, source_tiles, pair_lists, view_counts, disparities, conv_first, bias_first, conv_second, bias_second):
    strips = ref_features.reshape(STRIPS, ROWS, C, COLS)
    volume = lax.map(lambda packed: strip_variance(packed[0], packed[1], packed[2], source_tiles, disparities), (strips, pair_lists, view_counts))
    volume_wide = jnp.transpose(volume, (3, 1, 0, 2, 4)).reshape(1, C, PLANES, HEIGHT, COLS).astype(jnp.float32)
    kernel_one = jnp.transpose(conv_first, (2, 4, 0, 1, 3)).astype(jnp.float32)
    first_out = lax.conv_general_dilated(volume_wide, kernel_one, (1, 1, 1), ((1, 1), (1, 1), (1, 1)), dimension_numbers=("NCDHW", "OIDHW", "NCDHW"), precision=lax.Precision.HIGHEST)
    cost_first = jnp.maximum(first_out + bias_first[None, :, None, None, None], 0.0).astype(jnp.bfloat16)
    kernel_two = jnp.transpose(conv_second, (0, 4, 1, 2, 3)).astype(jnp.float32)
    second = lax.conv_general_dilated(cost_first.astype(jnp.float32), kernel_two, (2, 2, 2), ((1, 1), (1, 1), (1, 1)), dimension_numbers=("NCDHW", "OIDHW", "NCDHW"), precision=lax.Precision.HIGHEST)
    second = second + bias_second[None, :, None, None, None]
    return jnp.transpose(second[0], (1, 2, 0, 3))
```

```python
import functools

import jax
import jax.numpy as jnp
from jax import lax
from jax.experimental import pallas as pl
from jax.experimental.pallas import tpu as pltpu
from jax.sharding import PartitionSpec as P

MESH = pl.DeviceIdType.MESH


def requests(pair_ref, tiles_dev):
    _, sources, blocks = pair_ref.shape
    ids = [pair_ref[0, s, b] for s in range(sources) for b in range(blocks)]
    owners = [jnp.where(i >= 0, i // tiles_dev, -1) for i in ids]
    locals_ = [i - o * tiles_dev for i, o in zip(ids, owners)]
    ranks = []
    for at, owner in enumerate(owners):
        rank = jnp.int32(0)
        for before in range(at):
            rank = rank + jnp.where(owners[before] == owner, 1, 0)
        ranks.append(rank)
    return owners, locals_, ranks


def exchange_kernel(
    n_view, slot_cap, pair_ref, count_ref, disp_ref, tiles_hbm, ref_hbm,
    var_ref,
    wanted_ref, asked_ref, asked_smem, tiles_ref, ref_ref, wide_ref, stage_ref, arrived_refs,
    local_sem, ref_sem, smem_sem, ask_send, ask_recv, data_send, data_recv, halo_send, halo_recv,
):
    me = lax.axis_index("view")
    barrier = pltpu.get_barrier_semaphore()

    def greet(step, carry):
        peer = lax.rem(me + step, n_view)
        pl.semaphore_signal(barrier, inc=1, device_id={"view": peer}, device_id_type=MESH)
        return carry

    lax.fori_loop(1, n_view, greet, 0)
    tiles_dev, tile_rows, channels, n_cols = tiles_ref.shape
    fetch = pltpu.make_async_copy(tiles_hbm, tiles_ref, local_sem)
    fetch.start()
    fetch_ref = pltpu.make_async_copy(ref_hbm, ref_ref, ref_sem)
    fetch_ref.start()

    sources, planes = disp_ref.shape[1], disp_ref.shape[0]
    blocks = pair_ref.shape[2]
    rows_n = blocks * tile_rows
    owners, locals_, ranks = requests(pair_ref, tiles_dev)
    shape = (n_view, 1, 128)
    row = lax.broadcasted_iota(jnp.int32, shape, 0)
    lane = lax.broadcasted_iota(jnp.int32, shape, 2)
    table = jnp.zeros(shape, jnp.int32)
    for owner, local, rank in zip(owners, locals_, ranks):
        table = jnp.where((row == owner) & (lane == rank), local, table)
    wanted_ref[...] = table
    slots = [jnp.maximum(o * slot_cap + r, 0) for o, r in zip(owners, ranks)]

    def peer_at(step):
        side = 1 - 2 * lax.rem(step, 2)
        return lax.rem(me + n_view // 2 + side * ((step + 1) // 2) + n_view, n_view)

    pl.semaphore_wait(barrier, n_view - 1)

    def ask_copy(peer, into):
        return pltpu.make_async_remote_copy(
            src_ref=wanted_ref.at[peer],
            dst_ref=asked_ref.at[into],
            send_sem=ask_send.at[peer],
            recv_sem=ask_recv.at[into],
            device_id={"view": peer},
            device_id_type=MESH,
        )

    def ask(step, carry):
        ask_copy(peer_at(step), me).start()
        return carry

    lax.fori_loop(0, n_view - 1, ask, 0)
    asked_ref[me] = wanted_ref[me]

    @pl.when(me == 0)
    def _():
        var_ref[:, 0 : 2 * channels] = jnp.zeros((planes, 2 * channels, n_cols), var_ref.dtype)

    @pl.when(me == n_view - 1)
    def _():
        var_ref[:, (rows_n + 2) * channels :] = jnp.zeros((planes, channels, n_cols), var_ref.dtype)

    def answered(step, carry):
        peer = peer_at(step)
        copy = ask_copy(peer, peer)
        copy.wait_send()
        copy.wait_recv()
        return carry

    lax.fori_loop(0, n_view - 1, answered, 0)
    to_smem = pltpu.make_async_copy(asked_ref, asked_smem, smem_sem)
    to_smem.start()
    fetch.wait()
    to_smem.wait()

    parts = stage_ref.shape[0]
    halves = parts // tile_rows
    depth = channels // halves

    def data_copy(part, peer, into):
        return pltpu.make_async_remote_copy(
            src_ref=stage_ref.at[part, peer],
            dst_ref=arrived_refs[part].at[into],
            send_sem=data_send.at[part, peer],
            recv_sem=data_recv.at[part, into],
            device_id={"view": peer},
            device_id_type=MESH,
        )

    for part in range(parts):
        of_row, half = part // halves, part % halves

        def gather(step, carry):
            peer = peer_at(step)
            for slot in range(slot_cap):
                index = asked_smem[peer, 0, slot]
                stage_ref[part, peer, slot] = tiles_ref[
                    index, of_row, half * depth : (half + 1) * depth
                ]
            return carry

        def send(step, carry):
            data_copy(part, peer_at(step), me).start()
            return carry

        lax.fori_loop(0, n_view - 1, gather, 0)
        lax.fori_loop(0, n_view - 1, send, 0)
    for part in range(parts):
        of_row, half = part // halves, part % halves
        for slot in range(slot_cap):
            index = asked_smem[me, 0, slot]
            arrived_refs[part][me, slot] = tiles_ref[
                index, of_row, half * depth : (half + 1) * depth
            ]

    fetch_ref.wait()
    live = count_ref[0]
    total = live.astype(jnp.float32) + 1.0
    inverse = 1.0 / jnp.full((1, n_cols), total, jnp.float32)
    column = lax.broadcasted_iota(jnp.int32, (depth, n_cols), 1)

    def halo_copy(row_at, half, out_row, peer, at):
        return pltpu.make_async_remote_copy(
            src_ref=var_ref.at[:, pl.ds((row_at + 2) * channels + half * depth, depth)],
            dst_ref=var_ref.at[:, pl.ds(out_row * channels + half * depth, depth)],
            send_sem=halo_send.at[at, half],
            recv_sem=halo_recv.at[at, half],
            device_id={"view": peer},
            device_id_type=MESH,
        )

    up = jnp.maximum(me - 1, 0)
    down = jnp.minimum(me + 1, n_view - 1)

    def upward(half):
        return halo_copy(0, half, rows_n + 2, up, 0)

    def downward(half, which):
        return halo_copy(rows_n - 2 + which, half, which, down, 1 + which)

    for part in range(parts):
        of_row, half = part // halves, part % halves

        def settle(step, carry):
            peer = peer_at(step)
            data_copy(part, peer, peer).wait_recv()
            return carry

        lax.fori_loop(0, n_view - 1, settle, 0)
        order = [block * tile_rows + of_row for block in range(blocks)]
        if of_row == tile_rows - 1:
            order = order[::-1]
        for source in range(sources):
            for place, row_at in enumerate(order):
                slot = slots[source * blocks + row_at // tile_rows]
                tile = arrived_refs[part][slot // slot_cap, slot % slot_cap].astype(jnp.float32)
                wide_ref[source, place] = jnp.where(source < live, tile, 0.0)

        def one_plane(plane, carry):
            offsets = [disp_ref[plane, source] for source in range(sources)]
            for place, row_at in enumerate(order):
                summed = ref_ref[row_at, half * depth : (half + 1) * depth].astype(jnp.float32)
                squares = summed * summed
                for source in range(sources):
                    offset = offsets[source]
                    turned = pltpu.roll(
                        wide_ref[source, place], jnp.where(offset < 0, offset + n_cols, offset), 1
                    )
                    origin = column - offset
                    inside = (origin >= 0) & (origin < n_cols)
                    turned = jnp.where(inside, turned, 0.0)
                    summed = summed + turned
                    squares = squares + turned * turned
                mean = summed * inverse
                at = (row_at + 2) * channels + half * depth
                var_ref[plane, at : at + depth] = (squares * inverse - mean * mean).astype(
                    jnp.bfloat16
                )
            return carry

        lax.fori_loop(0, planes, one_plane, 0)
        if of_row == 0:
            pl.when(me > 0)(lambda: upward(half).start())
        if of_row == tile_rows - 2:
            pl.when(me < n_view - 1)(lambda: downward(half, 0).start())
        if of_row == tile_rows - 1:
            pl.when(me < n_view - 1)(lambda: downward(half, 1).start())

    def sent(step, carry):
        for part in range(parts):
            peer = peer_at(step)
            data_copy(part, peer, peer).wait_send()
        return carry

    lax.fori_loop(0, n_view - 1, sent, 0)

    @pl.when(me > 0)
    def _():
        for half in range(halves):
            upward(half).wait_send()
            downward(half, 0).wait_recv()
            downward(half, 1).wait_recv()

    @pl.when(me < n_view - 1)
    def _():
        for half in range(halves):
            downward(half, 0).wait_send()
            downward(half, 1).wait_send()
            upward(half).wait_recv()


def exchange(pair_lists, view_counts, disparities, source_tiles, ref_features):
    n_view = lax.axis_size("view")
    rows_n, channels, n_cols = ref_features.shape
    tiles_dev, tile_rows = source_tiles.shape[:2]
    _, sources, blocks = pair_lists.shape
    planes = disparities.shape[0]
    slot_cap = max(2, (sources * blocks + n_view - 1) // n_view)
    halves = 2
    parts = tile_rows * halves
    depth = channels // halves
    hbm = pl.BlockSpec(memory_space=pltpu.HBM)
    smem = pl.BlockSpec(memory_space=pltpu.SMEM)
    vmem = pl.BlockSpec(memory_space=pltpu.VMEM)
    return pl.pallas_call(
        functools.partial(exchange_kernel, n_view, slot_cap),
        out_shape=jax.ShapeDtypeStruct((planes, (rows_n + 3) * channels, n_cols), jnp.bfloat16),
        in_specs=[smem, smem, smem, hbm, hbm],
        out_specs=vmem,
        scratch_shapes=[
            pltpu.VMEM((n_view, 1, 128), jnp.int32),
            pltpu.VMEM((n_view, 1, 128), jnp.int32),
            pltpu.SMEM((n_view, 1, 128), jnp.int32),
            pltpu.VMEM(source_tiles.shape, jnp.bfloat16),
            pltpu.VMEM(ref_features.shape, jnp.bfloat16),
            pltpu.VMEM((sources, blocks, depth, n_cols), jnp.float32),
            pltpu.VMEM((parts, n_view, slot_cap, depth, n_cols), jnp.bfloat16),
            [pltpu.VMEM((n_view, slot_cap, depth, n_cols), jnp.bfloat16)] * parts,
            pltpu.SemaphoreType.DMA,
            pltpu.SemaphoreType.DMA,
            pltpu.SemaphoreType.DMA,
            pltpu.SemaphoreType.DMA((n_view,)),
            pltpu.SemaphoreType.DMA((n_view,)),
            pltpu.SemaphoreType.DMA((parts, n_view)),
            pltpu.SemaphoreType.DMA((parts, n_view)),
            pltpu.SemaphoreType.DMA((3, halves)),
            pltpu.SemaphoreType.DMA((3, halves)),
        ],
        compiler_params=pltpu.CompilerParams(
            collective_id=0, has_side_effects=True, vmem_limit_bytes=24 << 20
        ),
        name="exchange",
    )(pair_lists, view_counts, disparities, source_tiles, ref_features)


def prepare_kernel(first_ref, second_ref, bias1_ref, bias2_ref, w1_ref, w2_ref, b1_ref, b2_ref, pick_ref):
    taps_p, taps_r, c1, taps_x, channels = first_ref.shape
    rows_out = w1_ref.shape[0] // (taps_p * taps_x * c1)
    width = w1_ref.shape[1]
    lanes = -(-width // 128) * 128
    for a in range(taps_p):
        slabs = [first_ref[a, b].astype(jnp.float32) for b in range(taps_r)]
        for d in range(taps_x):
            pieces = [slab[:, d, :] for slab in slabs]
            rest = jnp.zeros((c1, lanes - taps_r * channels), jnp.float32)
            base = jnp.concatenate(pieces + [rest], axis=1)
            for hi in range(rows_out):
                band = pltpu.roll(base, hi * channels, 1) if hi else base
                at = ((a * taps_x + d) * rows_out + hi) * c1
                w1_ref[at : at + c1] = band[:, :width].astype(jnp.bfloat16)
    c2 = second_ref.shape[0]
    half_r = w2_ref.shape[0] // c2
    part = b1_ref.shape[0]
    columns = w2_ref.shape[1]
    spread = []
    for a in range(taps_p):
        slabs = [second_ref[:, a, b].astype(jnp.float32) for b in range(taps_r)]
        for d in range(taps_x):
            spread += [slab[:, d, :] for slab in slabs]
            spread.append(jnp.zeros((c2, part - taps_r * c1), jnp.float32))
    wide2 = -(-columns // 128) * 128
    if wide2 > columns:
        spread.append(jnp.zeros((c2, wide2 - columns), jnp.float32))
    base = jnp.concatenate(spread, axis=1)
    for g in range(half_r):
        band = pltpu.roll(base, 2 * g * c1, 1) if g else base
        w2_ref[g * c2 : (g + 1) * c2] = band[:, :columns].astype(jnp.bfloat16)
    row = lax.rem(lax.broadcasted_iota(jnp.int32, b1_ref.shape, 0), c1)
    b1 = jnp.zeros(b1_ref.shape, jnp.float32)
    for o in range(c1):
        b1 = jnp.where(row == o, bias1_ref[o], b1)
    b1_ref[...] = b1
    row = lax.rem(lax.broadcasted_iota(jnp.int32, b2_ref.shape, 0), c2)
    b2 = jnp.zeros(b2_ref.shape, jnp.float32)
    for k in range(c2):
        b2 = jnp.where(row == k, bias2_ref[k], b2)
    b2_ref[...] = b2
    n_cols = pick_ref.shape[0]
    wide = pick_ref.shape[1] // 3
    source = lax.broadcasted_iota(jnp.int32, (n_cols, wide), 0)
    target = lax.broadcasted_iota(jnp.int32, (n_cols, wide), 1)
    for tap in range(3):
        hit = (source == 2 * target + (tap - 1)) & (target < n_cols // 2)
        pick_ref[:, tap * wide : (tap + 1) * wide] = jnp.where(hit, 1.0, 0.0).astype(jnp.bfloat16)


def prepare(conv_first, conv_second, bias_first, bias_second, rows_n, n_cols, wide):
    taps_p, taps_r, c1, taps_x, channels = conv_first.shape
    c2 = conv_second.shape[0]
    half_rows = (rows_n + 2) // 2
    part = (rows_n + 2) * c1
    vmem = pl.BlockSpec(memory_space=pltpu.VMEM)
    smem = pl.BlockSpec(memory_space=pltpu.SMEM)
    return pl.pallas_call(
        prepare_kernel,
        out_shape=[
            jax.ShapeDtypeStruct(
                (taps_p * taps_x * half_rows * c1, (half_rows + 2) * channels), jnp.bfloat16
            ),
            jax.ShapeDtypeStruct((rows_n // 2 * c2, taps_p * taps_x * part), jnp.bfloat16),
            jax.ShapeDtypeStruct((part, 128), jnp.float32),
            jax.ShapeDtypeStruct((rows_n // 2 * c2, 128), jnp.float32),
            jax.ShapeDtypeStruct((n_cols, 3 * wide), jnp.bfloat16),
        ],
        in_specs=[vmem, vmem, smem, smem],
        out_specs=[vmem] * 5,
        compiler_params=pltpu.CompilerParams(vmem_limit_bytes=8 << 20),
        name="prepare",
    )(conv_first, conv_second, bias_first, bias_second)


def conv_kernel(
    var_ref, w1_ref, b1_ref, w2_ref, b2_ref, pick_ref, out_ref, acc_ref, cost_ref,
):
    planes, _, n_cols = var_ref.shape
    half = w1_ref.shape[0] // 9
    part = 2 * half
    depth = w1_ref.shape[1]
    half_p, half_r, c2, half_x = out_ref.shape
    wide = pick_ref.shape[1] // 3
    weights = w1_ref[...]

    def one_plane(plane):
        block = var_ref[plane]
        skip = depth // (half_r + 3) * (half_r + 1)
        lower = block[skip:]
        products = (
            jnp.dot(weights, block[:depth], preferred_element_type=jnp.float32),
            jnp.dot(weights[:, : lower.shape[0]], lower, preferred_element_type=jnp.float32),
        )
        for tap in range(3):
            target = plane + 1 - tap
            if 0 <= target < planes:
                for shift in range(3):
                    for side in range(2):
                        start = (tap * 3 + shift) * half
                        piece = products[side][start : start + half]
                        at = slice(shift * part + side * half, shift * part + (side + 1) * half)
                        if tap == 0 or (tap == 1 and plane == 0):
                            acc_ref[target, at] = piece
                        else:
                            acc_ref[target, at] += piece

    column = lax.broadcasted_iota(jnp.int32, (part, n_cols), 1)
    row = lax.broadcasted_iota(jnp.int32, (part, n_cols), 0)
    hidden = (row < part // (2 * half_r + 2)) & (lax.axis_index("view") == 0)
    cost_ref[0] = jnp.zeros(cost_ref.shape[1:], cost_ref.dtype)
    bias1 = b1_ref[:, 0:1]
    bias2 = b2_ref[:, 0:1]

    def finish(plane):
        left = jnp.where(column == 0, 0.0, pltpu.roll(acc_ref[plane, 0:part], 1, 1))
        right = jnp.where(
            column == n_cols - 1, 0.0, pltpu.roll(acc_ref[plane, 2 * part : 3 * part], n_cols - 1, 1)
        )
        total = acc_ref[plane, part : 2 * part] + left + right + bias1
        cost = jnp.where(hidden, 0.0, jnp.maximum(total, 0.0)).astype(jnp.bfloat16)
        spread = jnp.dot(cost, pick_ref[...], preferred_element_type=jnp.float32)
        spread = spread.astype(jnp.bfloat16)
        for tap in range(3):
            cost_ref[plane + 1, tap * part : (tap + 1) * part] = spread[
                :, tap * wide : (tap + 1) * wide
            ]

    def second(q):
        block = cost_ref[2 * q : 2 * q + 3].reshape(9 * part, wide)
        result = jnp.dot(w2_ref[...], block, preferred_element_type=jnp.float32)
        result = result + bias2
        out_ref[q] = result[:, :half_x].reshape(half_r, c2, half_x)

    for plane in range(planes):
        one_plane(plane)
        if plane >= 1:
            finish(plane - 1)
            if plane % 2 == 0:
                second(plane // 2 - 1)
    finish(planes - 1)
    second(half_p - 1)


def on_device(
    ref_features,
    source_tiles,
    pair_lists,
    view_counts,
    disparities,
    conv_first,
    bias_first,
    conv_second,
    bias_second,
):
    rows_n, channels, n_cols = ref_features.shape
    planes = disparities.shape[0]
    c1 = conv_first.shape[2]
    c2 = conv_second.shape[0]
    part = (rows_n + 2) * c1
    half_x = n_cols // 2
    wide = -(-half_x // 128) * 128
    weights = prepare(conv_first, conv_second, bias_first, bias_second, rows_n, n_cols, wide)
    w1, w2, b1, b2, pick = weights
    volume = exchange(pair_lists, view_counts, disparities, source_tiles, ref_features)
    vmem = pl.BlockSpec(memory_space=pltpu.VMEM)
    return pl.pallas_call(
        conv_kernel,
        out_shape=jax.ShapeDtypeStruct((planes // 2, rows_n // 2, c2, half_x), jnp.float32),
        in_specs=[vmem] * 6,
        out_specs=vmem,
        scratch_shapes=[
            pltpu.VMEM((planes, 3 * part, n_cols), jnp.float32),
            pltpu.VMEM((planes + 1, 3 * part, wide), jnp.bfloat16),
        ],
        compiler_params=pltpu.CompilerParams(vmem_limit_bytes=24 << 20),
        name="convolutions",
    )(volume, w1, b1, w2, b2, pick)


def solution(mesh):
    return jax.shard_map(
        on_device,
        mesh=mesh,
        in_specs=(
            P(("groups", "view"), None, None),
            P(("groups", "view"), None, None, None),
            P(("groups", "view"), None, None),
            P(("groups", "view")),
            P("groups", None),
            P(),
            P(),
            P(),
            P(),
        ),
        out_specs=P("groups", "view", None, None),
        check_vma=False,
    )
```

```python
import functools

import jax
import jax.numpy as jnp
from jax import lax
from jax.experimental import pallas as pl
from jax.experimental.pallas import tpu as pltpu
from jax.sharding import PartitionSpec as P

MESH = pl.DeviceIdType.MESH


def requests(pair_ref, tiles_dev):
    _, sources, blocks = pair_ref.shape
    ids = [pair_ref[0, s, b] for s in range(sources) for b in range(blocks)]
    owners = [jnp.where(i >= 0, i // tiles_dev, -1) for i in ids]
    locals_ = [i - o * tiles_dev for i, o in zip(ids, owners)]
    ranks = []
    for at, owner in enumerate(owners):
        rank = jnp.int32(0)
        for before in range(at):
            rank = rank + jnp.where(owners[before] == owner, 1, 0)
        ranks.append(rank)
    return owners, locals_, ranks


def prepare(first_ref, second_ref, bias1_ref, bias2_ref, own_refs, above_w, below_w, w2_ref, b1_ref, b2_ref, pick_ref):
    taps_p, taps_r, c1, taps_x, channels = first_ref.shape
    halves = len(own_refs) // 2
    depth = channels // halves
    rows_r = own_refs[0].shape[0] // (taps_x * c1)
    places = own_refs[0].shape[1] // (taps_p * depth)
    columns = taps_p * places * depth
    lanes = -(-columns // 128) * 128
    pieces = {}
    for a in range(taps_p):
        for b in range(taps_r):
            slab = first_ref[a, b].astype(jnp.float32)
            for d in range(taps_x):
                pieces[a, b, d] = slab[:, d, :]

    def zeros(rows, count):
        return jnp.zeros((rows, count), jnp.float32)

    for d in range(taps_x):
        for half in range(halves):
            cut = slice(half * depth, (half + 1) * depth)

            def base(taps):
                row = []
                for a in range(taps_p):
                    row += [zeros(c1, depth) if b is None else pieces[a, b, d][:, cut] for b in taps]
                    row.append(zeros(c1, (places - len(taps)) * depth))
                if lanes > columns:
                    row.append(zeros(c1, lanes - columns))
                return jnp.concatenate(row, axis=1)

            both, first, last, centre = base((0, 2)), base((0,)), base((2,)), base((1,))
            for parity in range(2):
                target = own_refs[parity * halves + half]
                for r in range(rows_r):
                    if (r - parity) % 2:
                        place = (r - 1 - parity) // 2
                        band = centre
                        inside = 0 <= place < places
                    else:
                        place = (r - 2 - parity) // 2
                        band = both
                        inside = True
                        if place < 0:
                            place, band, inside = place + 1, last, place + 1 == 0
                        elif place == places - 1:
                            band = first
                        elif place >= places:
                            inside = False
                    at = (d * rows_r + r) * c1
                    if not inside:
                        band = zeros(c1, columns)
                    elif place:
                        band = pltpu.roll(band, place * depth, 1)
                    target[at : at + c1] = band[:, :columns].astype(jnp.bfloat16)
        for r in range(2):
            row = []
            for a in range(taps_p):
                row += [pieces[a, 0, d], pieces[a, 1, d]] if r == 0 else [zeros(c1, channels), pieces[a, 0, d]]
            at = (d * 2 + r) * c1
            above_w[at : at + c1] = jnp.concatenate(row, axis=1).astype(jnp.bfloat16)
        row = [pieces[a, 2, d] for a in range(taps_p)]
        below_w[d * c1 : (d + 1) * c1] = jnp.concatenate(row, axis=1).astype(jnp.bfloat16)
    c2 = second_ref.shape[0]
    half_r = w2_ref.shape[0] // c2
    part = b1_ref.shape[0]
    columns = w2_ref.shape[1]
    spread = []
    for a in range(taps_p):
        slabs = [second_ref[:, a, b].astype(jnp.float32) for b in range(taps_r)]
        for d in range(taps_x):
            spread += [slab[:, d, :] for slab in slabs]
            spread.append(zeros(c2, part - taps_r * c1))
    wide2 = -(-columns // 128) * 128
    if wide2 > columns:
        spread.append(zeros(c2, wide2 - columns))
    base2 = jnp.concatenate(spread, axis=1)
    for g in range(half_r):
        band = pltpu.roll(base2, 2 * g * c1, 1) if g else base2
        w2_ref[g * c2 : (g + 1) * c2] = band[:, :columns].astype(jnp.bfloat16)
    row = lax.rem(lax.broadcasted_iota(jnp.int32, b1_ref.shape, 0), c1)
    b1 = jnp.zeros(b1_ref.shape, jnp.float32)
    for o in range(c1):
        b1 = jnp.where(row == o, bias1_ref[o], b1)
    b1_ref[...] = b1
    row = lax.rem(lax.broadcasted_iota(jnp.int32, b2_ref.shape, 0), c2)
    b2 = jnp.zeros(b2_ref.shape, jnp.float32)
    for k in range(c2):
        b2 = jnp.where(row == k, bias2_ref[k], b2)
    b2_ref[...] = b2
    n_cols = pick_ref.shape[0]
    wide = pick_ref.shape[1] // 3
    source = lax.broadcasted_iota(jnp.int32, (n_cols, wide), 0)
    target = lax.broadcasted_iota(jnp.int32, (n_cols, wide), 1)
    for tap in range(3):
        hit = (source == 2 * target + (tap - 1)) & (target < n_cols // 2)
        pick_ref[:, tap * wide : (tap + 1) * wide] = jnp.where(hit, 1.0, 0.0).astype(jnp.bfloat16)


def sweep_kernel(
    n_view, slot_cap, pair_ref, count_ref, disp_ref, bias1_ref, bias2_ref,
    tiles_hbm, ref_hbm, first_hbm, second_hbm,
    out_ref,
    wanted_ref, asked_ref, asked_smem, tiles_ref, ref_ref, first_ref, second_ref, wide_ref, stage_ref,
    arrived_refs, var_refs, above_ref, below_ref, own_refs, above_w, below_w, w2_ref, b1_ref, b2_ref,
    pick_ref, acc_ref, cost_ref,
    fetch_sem, smem_sem, ask_send, ask_recv, data_send, data_recv, halo_send, halo_recv,
):
    me = lax.axis_index("view")
    barrier = pltpu.get_barrier_semaphore()

    def greet(step, carry):
        peer = lax.rem(me + step, n_view)
        pl.semaphore_signal(barrier, inc=1, device_id={"view": peer}, device_id_type=MESH)
        return carry

    lax.fori_loop(1, n_view, greet, 0)
    tiles_dev, tile_rows, channels, n_cols = tiles_ref.shape
    pairs = ((tiles_hbm, tiles_ref), (ref_hbm, ref_ref), (first_hbm, first_ref), (second_hbm, second_ref))
    fetches = [
        pltpu.make_async_copy(src, dst, fetch_sem.at[at]) for at, (src, dst) in enumerate(pairs)
    ]
    for fetch in fetches:
        fetch.start()

    sources, planes = disp_ref.shape[1], disp_ref.shape[0]
    blocks = pair_ref.shape[2]
    owners, locals_, ranks = requests(pair_ref, tiles_dev)
    shape = (n_view, 1, 128)
    row = lax.broadcasted_iota(jnp.int32, shape, 0)
    lane = lax.broadcasted_iota(jnp.int32, shape, 2)
    table = jnp.zeros(shape, jnp.int32)
    for owner, local, rank in zip(owners, locals_, ranks):
        table = jnp.where((row == owner) & (lane == rank), local, table)
    wanted_ref[...] = table
    slots = [jnp.maximum(o * slot_cap + r, 0) for o, r in zip(owners, ranks)]

    def peer_at(step):
        side = 1 - 2 * lax.rem(step, 2)
        return lax.rem(me + n_view // 2 + side * ((step + 1) // 2) + n_view, n_view)

    pl.semaphore_wait(barrier, n_view - 1)

    def ask_copy(peer, into):
        return pltpu.make_async_remote_copy(
            src_ref=wanted_ref.at[peer],
            dst_ref=asked_ref.at[into],
            send_sem=ask_send.at[peer],
            recv_sem=ask_recv.at[into],
            device_id={"view": peer},
            device_id_type=MESH,
        )

    def ask(step, carry):
        ask_copy(peer_at(step), me).start()
        return carry

    lax.fori_loop(0, n_view - 1, ask, 0)
    asked_ref[me] = wanted_ref[me]

    @pl.when(me == 0)
    def _():
        above_ref[...] = jnp.zeros(above_ref.shape, above_ref.dtype)

    @pl.when(me == n_view - 1)
    def _():
        below_ref[...] = jnp.zeros(below_ref.shape, below_ref.dtype)

    for ref in (*var_refs, above_ref, below_ref):
        edge = jnp.zeros(ref.shape[1:], ref.dtype)
        ref[0] = edge
        ref[planes + 1] = edge
    cost_ref[0] = jnp.zeros(cost_ref.shape[1:], cost_ref.dtype)

    def answered(step, carry):
        peer = peer_at(step)
        copy = ask_copy(peer, peer)
        copy.wait_send()
        copy.wait_recv()
        return carry

    lax.fori_loop(0, n_view - 1, answered, 0)
    to_smem = pltpu.make_async_copy(asked_ref, asked_smem, smem_sem)
    to_smem.start()
    fetches[0].wait()
    to_smem.wait()

    parts = stage_ref.shape[0]
    halves = parts // tile_rows
    depth = channels // halves

    def data_copy(part, peer, into):
        return pltpu.make_async_remote_copy(
            src_ref=stage_ref.at[part, peer],
            dst_ref=arrived_refs[part].at[into],
            send_sem=data_send.at[part, peer],
            recv_sem=data_recv.at[part, into],
            device_id={"view": peer},
            device_id_type=MESH,
        )

    for part in range(parts):
        of_row, half = part // halves, part % halves

        def gather(step, carry):
            peer = peer_at(step)
            for slot in range(slot_cap):
                index = asked_smem[peer, 0, slot]
                stage_ref[part, peer, slot] = tiles_ref[
                    index, of_row, half * depth : (half + 1) * depth
                ]
            return carry

        def send(step, carry):
            data_copy(part, peer_at(step), me).start()
            return carry

        lax.fori_loop(0, n_view - 1, gather, 0)
        lax.fori_loop(0, n_view - 1, send, 0)
    for part in range(parts):
        of_row, half = part // halves, part % halves
        for slot in range(slot_cap):
            index = asked_smem[me, 0, slot]
            arrived_refs[part][me, slot] = tiles_ref[
                index, of_row, half * depth : (half + 1) * depth
            ]
    for fetch in fetches[1:]:
        fetch.wait()
    prepare(
        first_ref, second_ref, bias1_ref, bias2_ref, own_refs, above_w, below_w, w2_ref, b1_ref,
        b2_ref, pick_ref,
    )

    live = count_ref[0]
    total = live.astype(jnp.float32) + 1.0
    inverse = 1.0 / jnp.full((1, n_cols), total, jnp.float32)
    column = lax.broadcasted_iota(jnp.int32, (depth, n_cols), 1)
    up = jnp.maximum(me - 1, 0)
    down = jnp.minimum(me + 1, n_view - 1)

    def halo_copy(src, dst, at, half, peer):
        return pltpu.make_async_remote_copy(
            src_ref=src,
            dst_ref=dst,
            send_sem=halo_send.at[at, half],
            recv_sem=halo_recv.at[at, half],
            device_id={"view": peer},
            device_id_type=MESH,
        )

    own_planes = pl.ds(1, planes)
    bottom = pl.ds((blocks - 1) * depth, depth)

    def upward(half):
        return halo_copy(
            var_refs[half].at[own_planes, pl.ds(0, depth)],
            below_ref.at[own_planes, pl.ds(half * depth, depth)],
            0, half, up,
        )

    def downward(of_row, half):
        return halo_copy(
            var_refs[of_row * halves + half].at[own_planes, bottom],
            above_ref.at[own_planes, pl.ds(of_row * channels + half * depth, depth)],
            1 + of_row, half, down,
        )

    taps_x = 3
    piece_rows = acc_ref.shape[1] // taps_x
    c1 = above_w.shape[0] // (2 * taps_x)

    for part in range(parts):
        of_row, half = part // halves, part % halves

        def settle(step, carry):
            peer = peer_at(step)
            data_copy(part, peer, peer).wait_recv()
            return carry

        lax.fori_loop(0, n_view - 1, settle, 0)
        for source in range(sources):
            for place in range(blocks):
                slot = slots[source * blocks + place]
                tile = arrived_refs[part][slot // slot_cap, slot % slot_cap].astype(jnp.float32)
                wide_ref[source, place] = jnp.where(source < live, tile, 0.0)

        def variance(places):
            def one_plane(plane, carry):
                offsets = [disp_ref[plane, source] for source in range(sources)]
                for place in places:
                    row_at = place * tile_rows + of_row
                    summed = ref_ref[row_at, half * depth : (half + 1) * depth].astype(jnp.float32)
                    squares = summed * summed
                    for source in range(sources):
                        offset = offsets[source]
                        turned = pltpu.roll(
                            wide_ref[source, place],
                            jnp.where(offset < 0, offset + n_cols, offset),
                            1,
                        )
                        origin = column - offset
                        inside = (origin >= 0) & (origin < n_cols)
                        turned = jnp.where(inside, turned, 0.0)
                        summed = summed + turned
                        squares = squares + turned * turned
                    mean = summed * inverse
                    var_refs[part][plane + 1, place * depth : (place + 1) * depth] = (
                        squares * inverse - mean * mean
                    ).astype(jnp.bfloat16)
                return carry

            lax.fori_loop(0, planes, one_plane, 0)

        variance((0, blocks - 1))
        if of_row == 0:
            pl.when(me > 0)(lambda: upward(half).start())
        pl.when(me < n_view - 1)(lambda: downward(of_row, half).start())
        variance(tuple(range(1, blocks - 1)))
        weights = own_refs[part][...]
        for plane in range(planes):
            block = var_refs[part][plane : plane + 3].reshape(-1, n_cols)
            product = jnp.dot(weights, block, preferred_element_type=jnp.float32)
            if part == 0:
                acc_ref[plane] = product
            else:
                acc_ref[plane] += product
        if part == halves:
            @pl.when(me < n_view - 1)
            def _():
                for side in range(halves):
                    upward(side).wait_recv()

            weights = below_w[...]
            for plane in range(planes):
                block = below_ref[plane : plane + 3].reshape(-1, n_cols)
                product = jnp.dot(weights, block, preferred_element_type=jnp.float32)
                for tap in range(taps_x):
                    at = tap * piece_rows + blocks * tile_rows * c1
                    acc_ref[plane, at : at + c1] += product[tap * c1 : (tap + 1) * c1]

    @pl.when(me > 0)
    def _():
        for half in range(halves):
            for of_row in range(tile_rows):
                downward(of_row, half).wait_recv()

    half_p, half_r, c2, half_x = out_ref.shape
    wide = pick_ref.shape[1] // 3
    column = lax.broadcasted_iota(jnp.int32, (piece_rows, n_cols), 1)
    row = lax.broadcasted_iota(jnp.int32, (piece_rows, n_cols), 0)
    hidden = (row < c1) & (me == 0)
    bias1 = b1_ref[:, 0:1]
    bias2 = b2_ref[:, 0:1]

    def finish(plane):
        block = above_ref[plane : plane + 3].reshape(-1, n_cols)
        product = jnp.dot(above_w[...], block, preferred_element_type=jnp.float32)
        for tap in range(taps_x):
            at = tap * piece_rows
            acc_ref[plane, at : at + 2 * c1] += product[tap * 2 * c1 : (tap + 1) * 2 * c1]
        left = jnp.where(column == 0, 0.0, pltpu.roll(acc_ref[plane, 0:piece_rows], 1, 1))
        right = jnp.where(
            column == n_cols - 1,
            0.0,
            pltpu.roll(acc_ref[plane, 2 * piece_rows : 3 * piece_rows], n_cols - 1, 1),
        )
        total = acc_ref[plane, piece_rows : 2 * piece_rows] + left + right + bias1
        cost = jnp.where(hidden, 0.0, jnp.maximum(total, 0.0)).astype(jnp.bfloat16)
        spread = jnp.dot(cost, pick_ref[...], preferred_element_type=jnp.float32)
        spread = spread.astype(jnp.bfloat16)
        for tap in range(3):
            cost_ref[plane + 1, tap * piece_rows : (tap + 1) * piece_rows] = spread[
                :, tap * wide : (tap + 1) * wide
            ]

    def second(q):
        block = cost_ref[2 * q : 2 * q + 3].reshape(9 * piece_rows, wide)
        result = jnp.dot(w2_ref[...], block, preferred_element_type=jnp.float32)
        result = result + bias2
        out_ref[q] = result[:, :half_x].reshape(half_r, c2, half_x)

    for plane in range(planes):
        finish(plane)
        if plane % 2:
            second(plane // 2)

    def sent(step, carry):
        peer = peer_at(step)
        for part in range(parts):
            data_copy(part, peer, peer).wait_send()
        return carry

    lax.fori_loop(0, n_view - 1, sent, 0)

    @pl.when(me > 0)
    def _():
        for half in range(halves):
            upward(half).wait_send()

    @pl.when(me < n_view - 1)
    def _():
        for half in range(halves):
            for of_row in range(tile_rows):
                downward(of_row, half).wait_send()


def on_device(
    ref_features,
    source_tiles,
    pair_lists,
    view_counts,
    disparities,
    conv_first,
    bias_first,
    conv_second,
    bias_second,
):
    n_view = lax.axis_size("view")
    rows_n, channels, n_cols = ref_features.shape
    tiles_dev, tile_rows = source_tiles.shape[:2]
    _, sources, blocks = pair_lists.shape
    planes = disparities.shape[0]
    taps_p, _, c1, taps_x, _ = conv_first.shape
    c2 = conv_second.shape[0]
    slot_cap = max(2, (sources * blocks + n_view - 1) // n_view)
    halves = 2
    parts = tile_rows * halves
    depth = channels // halves
    part = (rows_n + 2) * c1
    half_x = n_cols // 2
    wide = -(-half_x // 128) * 128
    hbm = pl.BlockSpec(memory_space=pl.ANY)
    smem = pl.BlockSpec(memory_space=pltpu.SMEM)
    vmem = pl.BlockSpec(memory_space=pltpu.VMEM)
    bf16 = jnp.bfloat16
    return pl.pallas_call(
        functools.partial(sweep_kernel, n_view, slot_cap),
        out_shape=jax.ShapeDtypeStruct((planes // 2, rows_n // 2, c2, half_x), jnp.float32),
        in_specs=[smem] * 5 + [hbm] * 4,
        out_specs=vmem,
        scratch_shapes=[
            pltpu.VMEM((n_view, 1, 128), jnp.int32),
            pltpu.VMEM((n_view, 1, 128), jnp.int32),
            pltpu.SMEM((n_view, 1, 128), jnp.int32),
            pltpu.VMEM(source_tiles.shape, bf16),
            pltpu.VMEM(ref_features.shape, bf16),
            pltpu.VMEM(conv_first.shape, bf16),
            pltpu.VMEM(conv_second.shape, bf16),
            pltpu.VMEM((sources, blocks, depth, n_cols), jnp.float32),
            pltpu.VMEM((parts, n_view, slot_cap, depth, n_cols), bf16),
            [pltpu.VMEM((n_view, slot_cap, depth, n_cols), bf16)] * parts,
            [pltpu.VMEM((planes + 2, blocks * depth, n_cols), bf16)] * parts,
            pltpu.VMEM((planes + 2, 2 * channels, n_cols), bf16),
            pltpu.VMEM((planes + 2, channels, n_cols), bf16),
            [pltpu.VMEM((taps_x * part, taps_p * blocks * depth), bf16)] * parts,
            pltpu.VMEM((taps_x * 2 * c1, taps_p * 2 * channels), bf16),
            pltpu.VMEM((taps_x * c1, taps_p * channels), bf16),
            pltpu.VMEM((rows_n // 2 * c2, 9 * part), bf16),
            pltpu.VMEM((part, 128), jnp.float32),
            pltpu.VMEM((rows_n // 2 * c2, 128), jnp.float32),
            pltpu.VMEM((n_cols, 3 * wide), bf16),
            pltpu.VMEM((planes, taps_x * part, n_cols), jnp.float32),
            pltpu.VMEM((planes + 1, 3 * part, wide), bf16),
            pltpu.SemaphoreType.DMA((4,)),
            pltpu.SemaphoreType.DMA,
            pltpu.SemaphoreType.DMA((n_view,)),
            pltpu.SemaphoreType.DMA((n_view,)),
            pltpu.SemaphoreType.DMA((parts, n_view)),
            pltpu.SemaphoreType.DMA((parts, n_view)),
            pltpu.SemaphoreType.DMA((3, halves)),
            pltpu.SemaphoreType.DMA((3, halves)),
        ],
        compiler_params=pltpu.CompilerParams(
            collective_id=0, has_side_effects=True, vmem_limit_bytes=60 << 20
        ),
        name="sweep",
    )(
        pair_lists, view_counts, disparities, bias_first, bias_second,
        source_tiles, ref_features, conv_first, conv_second,
    )


def solution(mesh):
    return jax.shard_map(
        on_device,
        mesh=mesh,
        in_specs=(
            P(("groups", "view"), None, None),
            P(("groups", "view"), None, None, None),
            P(("groups", "view"), None, None),
            P(("groups", "view")),
            P("groups", None),
            P(),
            P(),
            P(),
            P(),
        ),
        out_specs=P("groups", "view", None, None),
        check_vma=False,
    )
```

```python
import functools

import jax
import jax.numpy as jnp
from jax import lax
from jax.experimental import pallas as pl
from jax.experimental.pallas import tpu as pltpu
from jax.sharding import PartitionSpec as P

MESH = pl.DeviceIdType.MESH


def requests(pair_ref, tiles_dev):
    _, sources, blocks = pair_ref.shape
    ids = [pair_ref[0, s, b] for s in range(sources) for b in range(blocks)]
    owners = [jnp.where(i >= 0, i // tiles_dev, -1) for i in ids]
    locals_ = [i - o * tiles_dev for i, o in zip(ids, owners)]
    ranks = []
    for at, owner in enumerate(owners):
        rank = jnp.int32(0)
        for before in range(at):
            rank = rank + jnp.where(owners[before] == owner, 1, 0)
        ranks.append(rank)
    return owners, locals_, ranks


def prepare(first_ref, second_ref, bias1_ref, bias2_ref, own_refs, above_w, below_w, w2_ref, b1_ref, b2_ref, pick_ref, turn_ref):
    taps_p, taps_r, taps_x, c1, channels = first_ref.shape
    halves = len(own_refs) // 2
    depth = channels // halves
    rows_r = own_refs[0].shape[0] // (taps_x * c1)
    places = own_refs[0].shape[1] // (taps_p * depth)
    columns = taps_p * places * depth
    lanes = -(-columns // 128) * 128
    pieces = {}
    for a in range(taps_p):
        for b in range(taps_r):
            for d in range(taps_x):
                pieces[a, b, d] = first_ref[a, b, d].astype(jnp.float32)

    def zeros(rows, count):
        return jnp.zeros((rows, count), jnp.float32)

    for d in range(taps_x):
        for half in range(halves):
            cut = slice(half * depth, (half + 1) * depth)

            def base(taps):
                row = []
                for a in range(taps_p):
                    row += [zeros(c1, depth) if b is None else pieces[a, b, d][:, cut] for b in taps]
                    row.append(zeros(c1, (places - len(taps)) * depth))
                if lanes > columns:
                    row.append(zeros(c1, lanes - columns))
                return jnp.concatenate(row, axis=1)

            both, first, last, centre = base((0, 2)), base((0,)), base((2,)), base((1,))
            for parity in range(2):
                target = own_refs[parity * halves + half]
                for r in range(rows_r):
                    if (r - parity) % 2:
                        place = (r - 1 - parity) // 2
                        band = centre
                        inside = 0 <= place < places
                    else:
                        place = (r - 2 - parity) // 2
                        band = both
                        inside = True
                        if place < 0:
                            place, band, inside = place + 1, last, place + 1 == 0
                        elif place == places - 1:
                            band = first
                        elif place >= places:
                            inside = False
                    at = (d * rows_r + r) * c1
                    if not inside:
                        band = zeros(c1, columns)
                    elif place:
                        band = pltpu.roll(band, place * depth, 1)
                    target[at : at + c1] = band[:, :columns].astype(jnp.bfloat16)
        for r in range(2):
            row = []
            for a in range(taps_p):
                row += [pieces[a, 0, d], pieces[a, 1, d]] if r == 0 else [zeros(c1, channels), pieces[a, 0, d]]
            at = (d * 2 + r) * c1
            above_w[at : at + c1] = jnp.concatenate(row, axis=1).astype(jnp.bfloat16)
        row = [pieces[a, 2, d] for a in range(taps_p)]
        below_w[d * c1 : (d + 1) * c1] = jnp.concatenate(row, axis=1).astype(jnp.bfloat16)
    c2 = second_ref.shape[-1]
    half_r = w2_ref.shape[0] // c2
    part = b1_ref.shape[0]
    columns = w2_ref.shape[1]
    turn_ref[...] = jnp.zeros(turn_ref.shape, jnp.float32)
    for a in range(taps_p):
        for d in range(taps_x):
            for b in range(taps_r):
                at = (a * taps_x + d) * part + b * c1
                turn_ref[at : at + c1, 0:c2] = second_ref[a, b, d].astype(jnp.float32)
    base2 = turn_ref[...].T[:c2]
    for g in range(half_r):
        band = pltpu.roll(base2, 2 * g * c1, 1) if g else base2
        w2_ref[g * c2 : (g + 1) * c2] = band[:, :columns].astype(jnp.bfloat16)
    row = lax.rem(lax.broadcasted_iota(jnp.int32, b1_ref.shape, 0), c1)
    b1 = jnp.zeros(b1_ref.shape, jnp.float32)
    for o in range(c1):
        b1 = jnp.where(row == o, bias1_ref[o], b1)
    b1_ref[...] = b1
    row = lax.rem(lax.broadcasted_iota(jnp.int32, b2_ref.shape, 0), c2)
    b2 = jnp.zeros(b2_ref.shape, jnp.float32)
    for k in range(c2):
        b2 = jnp.where(row == k, bias2_ref[k], b2)
    b2_ref[...] = b2
    n_cols = pick_ref.shape[0]
    wide = pick_ref.shape[1] // 3
    source = lax.broadcasted_iota(jnp.int32, (n_cols, wide), 0)
    target = lax.broadcasted_iota(jnp.int32, (n_cols, wide), 1)
    for tap in range(3):
        hit = (source == 2 * target + (tap - 1)) & (target < n_cols // 2)
        pick_ref[:, tap * wide : (tap + 1) * wide] = jnp.where(hit, 1.0, 0.0).astype(jnp.bfloat16)


def sweep_kernel(
    n_view, slot_cap, pair_ref, count_ref, turned_disp_ref, bias1_ref, bias2_ref,
    tiles_hbm, ref_hbm, first_hbm, second_hbm,
    out_ref,
    wanted_ref, asked_ref, asked_smem, tiles_ref, ref_ref, first_ref, second_ref, wide_ref, stage_ref,
    arrived_refs, var_refs, above_ref, below_ref, own_refs, above_w, below_w, w2_ref, b1_ref, b2_ref,
    pick_ref, turn_ref, acc_ref, cost_ref,
    fetch_sem, smem_sem, ask_send, ask_recv, data_send, data_recv, halo_send, halo_recv,
):
    me = lax.axis_index("view")
    barrier = pltpu.get_barrier_semaphore()

    def greet(step, carry):
        peer = lax.rem(me + step, n_view)
        pl.semaphore_signal(barrier, inc=1, device_id={"view": peer}, device_id_type=MESH)
        return carry

    lax.fori_loop(1, n_view, greet, 0)
    tiles_dev, tile_rows, channels, n_cols = tiles_ref.shape
    pairs = ((tiles_hbm, tiles_ref), (ref_hbm, ref_ref), (first_hbm, first_ref), (second_hbm, second_ref))
    fetches = [
        pltpu.make_async_copy(src, dst, fetch_sem.at[at]) for at, (src, dst) in enumerate(pairs)
    ]
    for fetch in fetches:
        fetch.start()

    sources, planes = turned_disp_ref.shape
    blocks = pair_ref.shape[2]
    owners, locals_, ranks = requests(pair_ref, tiles_dev)
    shape = (n_view, 1, 128)
    row = lax.broadcasted_iota(jnp.int32, shape, 0)
    lane = lax.broadcasted_iota(jnp.int32, shape, 2)
    table = jnp.zeros(shape, jnp.int32)
    for owner, local, rank in zip(owners, locals_, ranks):
        table = jnp.where((row == owner) & (lane == rank), local, table)
    wanted_ref[...] = table
    slots = [jnp.maximum(o * slot_cap + r, 0) for o, r in zip(owners, ranks)]

    def peer_at(step):
        side = 1 - 2 * lax.rem(step, 2)
        return lax.rem(me + n_view // 2 + side * ((step + 1) // 2) + n_view, n_view)

    pl.semaphore_wait(barrier, n_view - 1)

    def ask_copy(peer, into):
        return pltpu.make_async_remote_copy(
            src_ref=wanted_ref.at[peer],
            dst_ref=asked_ref.at[into],
            send_sem=ask_send.at[peer],
            recv_sem=ask_recv.at[into],
            device_id={"view": peer},
            device_id_type=MESH,
        )

    def ask(step, carry):
        ask_copy(peer_at(step), me).start()
        return carry

    lax.fori_loop(0, n_view - 1, ask, 0)
    asked_ref[me] = wanted_ref[me]

    @pl.when(me == 0)
    def _():
        above_ref[...] = jnp.zeros(above_ref.shape, above_ref.dtype)

    @pl.when(me == n_view - 1)
    def _():
        below_ref[...] = jnp.zeros(below_ref.shape, below_ref.dtype)

    for ref in (*var_refs, above_ref, below_ref):
        edge = jnp.zeros(ref.shape[1:], ref.dtype)
        ref[0] = edge
        ref[planes + 1] = edge
    cost_ref[0] = jnp.zeros(cost_ref.shape[1:], cost_ref.dtype)

    def answered(step, carry):
        peer = peer_at(step)
        copy = ask_copy(peer, peer)
        copy.wait_send()
        copy.wait_recv()
        return carry

    lax.fori_loop(0, n_view - 1, answered, 0)
    to_smem = pltpu.make_async_copy(asked_ref, asked_smem, smem_sem)
    to_smem.start()
    fetches[0].wait()
    to_smem.wait()

    parts = stage_ref.shape[0]
    halves = parts // tile_rows
    depth = channels // halves

    def data_copy(part, peer, into):
        return pltpu.make_async_remote_copy(
            src_ref=stage_ref.at[part, peer],
            dst_ref=arrived_refs[part].at[into],
            send_sem=data_send.at[part, peer],
            recv_sem=data_recv.at[part, into],
            device_id={"view": peer},
            device_id_type=MESH,
        )

    for part in range(parts):
        of_row, half = part // halves, part % halves

        def gather(step, carry):
            peer = peer_at(step)
            for slot in range(slot_cap):
                index = asked_smem[peer, 0, slot]
                stage_ref[part, peer, slot] = tiles_ref[
                    index, of_row, half * depth : (half + 1) * depth
                ]
            return carry

        def send(step, carry):
            data_copy(part, peer_at(step), me).start()
            return carry

        lax.fori_loop(0, n_view - 1, gather, 0)
        lax.fori_loop(0, n_view - 1, send, 0)
    for part in range(parts):
        of_row, half = part // halves, part % halves
        for slot in range(slot_cap):
            index = asked_smem[me, 0, slot]
            arrived_refs[part][me, slot] = tiles_ref[
                index, of_row, half * depth : (half + 1) * depth
            ]
    for fetch in fetches[1:]:
        fetch.wait()
    prepare(
        first_ref, second_ref, bias1_ref, bias2_ref, own_refs, above_w, below_w, w2_ref, b1_ref,
        b2_ref, pick_ref, turn_ref,
    )

    live = count_ref[0]
    total = live.astype(jnp.float32) + 1.0
    inverse = 1.0 / jnp.full((1, n_cols), total, jnp.float32)
    column = lax.broadcasted_iota(jnp.int32, (depth, n_cols), 1)
    up = jnp.maximum(me - 1, 0)
    down = jnp.minimum(me + 1, n_view - 1)

    def halo_copy(src, dst, at, half, peer):
        return pltpu.make_async_remote_copy(
            src_ref=src,
            dst_ref=dst,
            send_sem=halo_send.at[at, half],
            recv_sem=halo_recv.at[at, half],
            device_id={"view": peer},
            device_id_type=MESH,
        )

    own_planes = pl.ds(1, planes)
    bottom = pl.ds((blocks - 1) * depth, depth)

    def upward(half):
        return halo_copy(
            var_refs[half].at[own_planes, pl.ds(0, depth)],
            below_ref.at[own_planes, pl.ds(half * depth, depth)],
            0, half, up,
        )

    def downward(of_row, half):
        return halo_copy(
            var_refs[of_row * halves + half].at[own_planes, bottom],
            above_ref.at[own_planes, pl.ds(of_row * channels + half * depth, depth)],
            1 + of_row, half, down,
        )

    taps_x = 3
    piece_rows = acc_ref.shape[1] // taps_x
    c1 = above_w.shape[0] // (2 * taps_x)

    for part in range(parts):
        of_row, half = part // halves, part % halves

        def settle(step, carry):
            peer = peer_at(step)
            data_copy(part, peer, peer).wait_recv()
            return carry

        lax.fori_loop(0, n_view - 1, settle, 0)
        for source in range(sources):
            for place in range(blocks):
                slot = slots[source * blocks + place]
                tile = arrived_refs[part][slot // slot_cap, slot % slot_cap].astype(jnp.float32)
                wide_ref[source, place] = jnp.where(source < live, tile, 0.0)

        def variance(places):
            def one_plane(plane, carry):
                offsets = [turned_disp_ref[source, plane] for source in range(sources)]
                for place in places:
                    row_at = place * tile_rows + of_row
                    summed = ref_ref[row_at, half * depth : (half + 1) * depth].astype(jnp.float32)
                    squares = summed * summed
                    for source in range(sources):
                        offset = offsets[source]
                        turned = pltpu.roll(
                            wide_ref[source, place],
                            jnp.where(offset < 0, offset + n_cols, offset),
                            1,
                        )
                        origin = column - offset
                        inside = (origin >= 0) & (origin < n_cols)
                        turned = jnp.where(inside, turned, 0.0)
                        summed = summed + turned
                        squares = squares + turned * turned
                    mean = summed * inverse
                    var_refs[part][plane + 1, place * depth : (place + 1) * depth] = (
                        squares * inverse - mean * mean
                    ).astype(jnp.bfloat16)
                return carry

            lax.fori_loop(0, planes, one_plane, 0)

        variance((0, blocks - 1))
        if of_row == 0:
            pl.when(me > 0)(lambda: upward(half).start())
        pl.when(me < n_view - 1)(lambda: downward(of_row, half).start())
        variance(tuple(range(1, blocks - 1)))
        weights = own_refs[part][...]
        for plane in range(planes):
            block = var_refs[part][plane : plane + 3].reshape(-1, n_cols)
            product = jnp.dot(weights, block, preferred_element_type=jnp.float32)
            if part == 0:
                acc_ref[plane] = product
            else:
                acc_ref[plane] += product
        if part == halves:
            @pl.when(me < n_view - 1)
            def _():
                for side in range(halves):
                    upward(side).wait_recv()

            weights = below_w[...]
            for plane in range(planes):
                block = below_ref[plane : plane + 3].reshape(-1, n_cols)
                product = jnp.dot(weights, block, preferred_element_type=jnp.float32)
                for tap in range(taps_x):
                    at = tap * piece_rows + blocks * tile_rows * c1
                    acc_ref[plane, at : at + c1] += product[tap * c1 : (tap + 1) * c1]

    @pl.when(me > 0)
    def _():
        for half in range(halves):
            for of_row in range(tile_rows):
                downward(of_row, half).wait_recv()

    half_p, half_r, c2, half_x = out_ref.shape
    wide = pick_ref.shape[1] // 3
    column = lax.broadcasted_iota(jnp.int32, (piece_rows, n_cols), 1)
    row = lax.broadcasted_iota(jnp.int32, (piece_rows, n_cols), 0)
    hidden = (row < c1) & (me == 0)
    bias1 = b1_ref[:, 0:1]
    bias2 = b2_ref[:, 0:1]

    def finish(plane):
        block = above_ref[plane : plane + 3].reshape(-1, n_cols)
        product = jnp.dot(above_w[...], block, preferred_element_type=jnp.float32)
        for tap in range(taps_x):
            at = tap * piece_rows
            acc_ref[plane, at : at + 2 * c1] += product[tap * 2 * c1 : (tap + 1) * 2 * c1]
        left = jnp.where(column == 0, 0.0, pltpu.roll(acc_ref[plane, 0:piece_rows], 1, 1))
        right = jnp.where(
            column == n_cols - 1,
            0.0,
            pltpu.roll(acc_ref[plane, 2 * piece_rows : 3 * piece_rows], n_cols - 1, 1),
        )
        total = acc_ref[plane, piece_rows : 2 * piece_rows] + left + right + bias1
        cost = jnp.where(hidden, 0.0, jnp.maximum(total, 0.0)).astype(jnp.bfloat16)
        spread = jnp.dot(cost, pick_ref[...], preferred_element_type=jnp.float32)
        spread = spread.astype(jnp.bfloat16)
        for tap in range(3):
            cost_ref[plane + 1, tap * piece_rows : (tap + 1) * piece_rows] = spread[
                :, tap * wide : (tap + 1) * wide
            ]

    def second(q):
        block = cost_ref[2 * q : 2 * q + 3].reshape(9 * piece_rows, wide)
        result = jnp.dot(w2_ref[...], block, preferred_element_type=jnp.float32)
        result = result + bias2
        out_ref[q] = result[:, :half_x].reshape(half_r, c2, half_x)

    for plane in range(planes):
        finish(plane)
        if plane % 2:
            second(plane // 2)

    def sent(step, carry):
        peer = peer_at(step)
        for part in range(parts):
            data_copy(part, peer, peer).wait_send()
        return carry

    lax.fori_loop(0, n_view - 1, sent, 0)

    @pl.when(me > 0)
    def _():
        for half in range(halves):
            upward(half).wait_send()

    @pl.when(me < n_view - 1)
    def _():
        for half in range(halves):
            for of_row in range(tile_rows):
                downward(of_row, half).wait_send()


def on_device(
    ref_features,
    source_tiles,
    pair_lists,
    view_counts,
    disparities,
    conv_first,
    bias_first,
    conv_second,
    bias_second,
):
    n_view = lax.axis_size("view")
    rows_n, channels, n_cols = ref_features.shape
    tiles_dev, tile_rows = source_tiles.shape[:2]
    _, sources, blocks = pair_lists.shape
    planes = disparities.shape[0]
    taps_p, _, c1, taps_x, _ = conv_first.shape
    c2 = conv_second.shape[0]
    turned_first = jnp.transpose(conv_first, (0, 1, 3, 2, 4))
    turned_second = jnp.transpose(conv_second, (1, 2, 3, 4, 0))
    slot_cap = max(2, (sources * blocks + n_view - 1) // n_view)
    halves = 2
    parts = tile_rows * halves
    depth = channels // halves
    part = (rows_n + 2) * c1
    half_x = n_cols // 2
    wide = -(-half_x // 128) * 128
    hbm = pl.BlockSpec(memory_space=pl.ANY)
    smem = pl.BlockSpec(memory_space=pltpu.SMEM)
    vmem = pl.BlockSpec(memory_space=pltpu.VMEM)
    bf16 = jnp.bfloat16
    return pl.pallas_call(
        functools.partial(sweep_kernel, n_view, slot_cap),
        out_shape=jax.ShapeDtypeStruct((planes // 2, rows_n // 2, c2, half_x), jnp.float32),
        in_specs=[smem] * 5 + [hbm] * 4,
        out_specs=vmem,
        scratch_shapes=[
            pltpu.VMEM((n_view, 1, 128), jnp.int32),
            pltpu.VMEM((n_view, 1, 128), jnp.int32),
            pltpu.SMEM((n_view, 1, 128), jnp.int32),
            pltpu.VMEM(source_tiles.shape, bf16),
            pltpu.VMEM(ref_features.shape, bf16),
            pltpu.VMEM(turned_first.shape, bf16),
            pltpu.VMEM(turned_second.shape, bf16),
            pltpu.VMEM((sources, blocks, depth, n_cols), jnp.float32),
            pltpu.VMEM((parts, n_view, slot_cap, depth, n_cols), bf16),
            [pltpu.VMEM((n_view, slot_cap, depth, n_cols), bf16)] * parts,
            [pltpu.VMEM((planes + 2, blocks * depth, n_cols), bf16)] * parts,
            pltpu.VMEM((planes + 2, 2 * channels, n_cols), bf16),
            pltpu.VMEM((planes + 2, channels, n_cols), bf16),
            [pltpu.VMEM((taps_x * part, taps_p * blocks * depth), bf16)] * parts,
            pltpu.VMEM((taps_x * 2 * c1, taps_p * 2 * channels), bf16),
            pltpu.VMEM((taps_x * c1, taps_p * channels), bf16),
            pltpu.VMEM((rows_n // 2 * c2, 9 * part), bf16),
            pltpu.VMEM((part, 128), jnp.float32),
            pltpu.VMEM((rows_n // 2 * c2, 128), jnp.float32),
            pltpu.VMEM((n_cols, 3 * wide), bf16),
            pltpu.VMEM((-(-9 * part // 128) * 128, 128), jnp.float32),
            pltpu.VMEM((planes, taps_x * part, n_cols), jnp.float32),
            pltpu.VMEM((planes + 1, 3 * part, wide), bf16),
            pltpu.SemaphoreType.DMA((4,)),
            pltpu.SemaphoreType.DMA,
            pltpu.SemaphoreType.DMA((n_view,)),
            pltpu.SemaphoreType.DMA((n_view,)),
            pltpu.SemaphoreType.DMA((parts, n_view)),
            pltpu.SemaphoreType.DMA((parts, n_view)),
            pltpu.SemaphoreType.DMA((3, halves)),
            pltpu.SemaphoreType.DMA((3, halves)),
        ],
        compiler_params=pltpu.CompilerParams(
            collective_id=0, has_side_effects=True, vmem_limit_bytes=60 << 20
        ),
        name="sweep",
    )(
        pair_lists, view_counts, disparities.T, bias_first, bias_second,
        source_tiles, ref_features, turned_first, turned_second,
    )


def solution(mesh):
    return jax.shard_map(
        on_device,
        mesh=mesh,
        in_specs=(
            P(("groups", "view"), None, None),
            P(("groups", "view"), None, None, None),
            P(("groups", "view"), None, None),
            P(("groups", "view")),
            P("groups", None),
            P(),
            P(),
            P(),
            P(),
        ),
        out_specs=P("groups", "view", None, None),
        check_vma=False,
    )
```
